32 devices in a mesh: dp: 2 (over x), expert: 16 (over z, y, core).
Axes of the slice: x: 2, y: 2, z: 4, core: 2. Of those that a mesh axis runs over, the one named last changes fastest.
Arguments:
- out_grad: bfloat16 [4096, 1040], P(('dp', 'expert')), may hold values from -8 to 8
- routes: int32 [4096, 1], P(('dp', 'expert')), may hold values from 0 to 15; in each aligned block of 128 rows (0 to 127, 128 to 255, ...) at most 12 rows name the same one
- pre_act: bfloat16 [6144, 3072], P(('dp', 'expert')), may hold values from -6 to 6
- out_weight: bfloat16 [16, 3072, 1040], P('expert', 'dp'), may hold values from -0.109375 to 0.109375
- row_factor: float32 [16, 3072], P('expert', 'dp'), may hold values from 1 to 100
- col_factor: float32 [16, 1040], P('expert'), may hold values from 1 to 100
Outputs:
- hidden_grad: bfloat16 [4096, 3072], P(('dp', 'expert'))
- new_weight: bfloat16 [16, 3072, 1040], P('expert', 'dp')
- new_row: float32 [16, 3072], P('expert', 'dp')
- new_col: float32 [16, 1040], P('expert')
The draws below stay inside these ranges and needn't reach their ends.
Inputs may be any that keep to these rules, and one draw needn't show every extreme that they name: `routes`: in the rows of one device no expert is named by more than 12 rows.
All inputs are finite; a program needn't handle non-finite values.
Results may differ from the reference program's by a relative error of at most 0.0025.
Values may be sent and summed in bfloat16 or wider, within the bound.
A program may use at most 64 MiB of HBM per device.

```python
import math
import jax
import jax.numpy as jnp
import numpy as np
from jax import lax

D = 1040
FF = 3072
TOK_DEV = 128
EXPERTS = 16
SLOT = 12
R = 192
TOKENS = 4096
N_DP = 2
N_EXPERT = 16


def draw_out_grad(key, part):
    key_scale, key_base = jax.random.split(jax.random.fold_in(key, 11))
    levels = jnp.exp(jax.random.uniform(key_scale, (N_DP, 1, D), jnp.float32, math.log(0.3), math.log(3.2)))
    base_value = jax.random.normal(key_base, (N_DP, TOKENS // N_DP, D), jnp.float32)
    shaped = jnp.clip(base_value * levels, -8.0, 8.0)
    return shaped.reshape(TOKENS, D).astype(jnp.bfloat16)


def draw_pre_act(key, part):
    slot_rows = N_EXPERT * R
    blocks = 64
    key_level, key_base = jax.random.split(jax.random.fold_in(key, 23), 2)
    levels = jnp.exp(jax.random.uniform(key_level, (N_DP, 1, blocks, 1), jnp.float32, -1.2 * math.log(10.0), 0.5 * math.log(10.0)))
    base_value = jax.random.normal(key_base, (N_DP, slot_rows, blocks, FF // blocks), jnp.float32)
    shaped = jnp.clip(base_value * levels, -6.0, 6.0)
    return shaped.reshape(N_DP * slot_rows, FF).astype(jnp.bfloat16)


def level_of(stream_key, extent, pieces, smallest, largest):
    def one(axis_at, parts):
        draws = jax.random.uniform(jax.random.fold_in(jax.random.fold_in(stream_key, 6), axis_at), (parts,), jnp.float32, smallest / len(pieces), largest / len(pieces))
        return jnp.repeat(jnp.exp(draws), extent[axis_at] // parts).reshape((-1,) + (1,) * (len(extent) - axis_at - 1))

    loudness = one(*pieces[0])
    for cut in pieces[1:]:
        loudness = loudness * one(*cut)
    return loudness


def routed_block(own_key, own, number, rows, amount, top, reach, slope):
    order = jax.random.permutation(own_key, amount)
    heavy_load, ordinary = shares(amount, rows * top, reach, slope, True), shares(amount, rows * top, reach, slope, False)
    places = jnp.arange(amount)

    def named(lengths, rotation):
        used = int((lengths > 0).sum())
        fixed = max(1, used // 4)
        moved = fixed + (places - fixed + rotation * (used - fixed)) % max(1, amount - fixed)
        return jnp.zeros((amount,), jnp.int32).at[order[jnp.where(places < fixed, places, moved)]].set(jnp.asarray(lengths, jnp.int32))

    lengths = jnp.where(number % 4 == 0, named(heavy_load, number // 4), named(ordinary, number - number // 4 - 1))
    mixed = jax.random.permutation(jax.random.fold_in(own, 3), amount)
    source_of, taker = mixed[0:amount // 2 * 2:2], mixed[1:amount // 2 * 2:2]
    room = jnp.minimum(lengths[source_of] - 1, reach - lengths[taker]) // 2
    room = jnp.where((source_of == order[0]) | (taker == order[0]) | (lengths[taker] == 0), 0, jnp.maximum(room, 0))
    moved = jax.random.randint(jax.random.fold_in(own, 4), (amount // 2,), 0, 1 << 20) % (room + 1)
    lengths = lengths.at[source_of].add(-moved).at[taker].add(moved)
    members = jnp.searchsorted(jnp.cumsum(lengths), jnp.arange(rows * top), side="right").astype(jnp.int32)
    listing = members.reshape(top, rows).T
    listing = listing[jax.random.permutation(jax.random.fold_in(own, 1), rows)]
    rotation = jax.random.randint(jax.random.fold_in(own, 2), (rows, 1), 0, top)
    return jnp.take_along_axis(listing, (jnp.arange(top)[None, :] + rotation) % top, axis=1)


def shares(count, total, limit, lean, full):
    weights = [(1 << 20) // math.isqrt(rank ** lean) + 1 for rank in range(1, count + 1)]
    largest = limit if full else min(limit, max(-(-total // count), total * weights[0] // sum(weights)))
    least = 1 if total - largest >= count - 1 else 0
    given, surplus = [largest] + [least] * (count - 1), total - largest - least * (count - 1)
    while surplus > 0:
        free = [i for i in range(1, count) if given[i] < largest] or [i for i in range(1, count) if given[i] < limit]
        pool, remaining = sum([weights[i] for i in free]), surplus
        for i in free:
            extra = min(limit - given[i], max(1, remaining * weights[i] // pool), surplus)
            given[i] = given[i] + extra
            surplus = surplus - extra
    return np.array(given)


def noise(rng, extent, scale, bound, cuts=(), kind=jnp.bfloat16):
    values = scale * jax.random.normal(rng, extent, jnp.float32)
    if cuts:
        values = values * level_of(rng, extent, cuts, -0.22, 0.18)
    return jnp.clip(values, -bound, bound).astype(kind)


def setup_inputs(seed: int = 0) -> dict:
    key_of = jax.random.split(jax.random.key(seed), 7)
    out_grad = draw_out_grad(jax.random.fold_in(key_of[6], 71), 0)
    routes_keys = jax.random.split(jax.random.fold_in(key_of[1], 1), TOKENS // TOK_DEV)
    routes_turns = jax.random.permutation(jax.random.fold_in(key_of[1], 3), TOKENS // TOK_DEV)
    routes = jax.vmap(lambda own, number: routed_block(jax.random.fold_in(key_of[1], 2), own, number, TOK_DEV, EXPERTS, 1, SLOT, 2))(routes_keys, routes_turns).reshape((TOKENS, 1))
    pre_act = draw_pre_act(jax.random.fold_in(key_of[6], 71), 0)
    out_weight = noise(key_of[3], (EXPERTS, FF, D), FF ** -0.5, 0.109375, ((0, 16), (1, 2)))
    row_factor = jnp.clip(jnp.exp(math.log(100.0) - 4.6051702 * jax.random.uniform(key_of[4], (EXPERTS, FF), jnp.float32) ** level_of(key_of[4], (EXPERTS, FF), ((0, 16), (1, 2)), -0.2, 0.2)), 1.0, 100.0)
    col_factor = jnp.clip(jnp.exp(math.log(100.0) - 4.6051702 * jax.random.uniform(key_of[5], (EXPERTS, D), jnp.float32) ** level_of(key_of[5], (EXPERTS, D), ((0, 16),), -0.2, 0.2)), 1.0, 100.0)
    return {"out_grad": out_grad, "routes": routes, "pre_act": pre_act, "out_weight": out_weight, "row_factor": row_factor, "col_factor": col_factor}


def slot_of(routes):
    blocks = routes.reshape(N_DP * N_EXPERT, TOK_DEV)
    same = blocks[:, :, None] == blocks[:, None, :]
    earlier = jnp.arange(TOK_DEV)[None, :] < jnp.arange(TOK_DEV)[:, None]
    order_in = lax.optimization_barrier(jnp.sum((same & earlier[None]).astype(jnp.int32), axis=2)).astype(jnp.int32)
    return (blocks * SLOT + order_in).astype(jnp.int32)

def expert_step(items):
    dy_rows, pre_rows, weight, row_old, col_old = items
    weight_f = weight.astype(jnp.float32)
    back_f = jnp.dot(dy_rows.astype(jnp.float32), weight_f.T)
    back = jnp.where(pre_rows > 0, back_f, 0.0).astype(jnp.bfloat16)
    hidden = jnp.maximum(pre_rows, 0).astype(jnp.float32)
    gradient = jnp.dot(hidden.T, dy_rows.astype(jnp.float32))
    squares = gradient * gradient + 1e-30
    row_new = 0.8 * row_old + 0.2 * lax.optimization_barrier(jnp.mean(squares, axis=1))
    col_new = 0.8 * col_old + 0.2 * lax.optimization_barrier(jnp.mean(squares, axis=0))
    second = row_new[:, None] * col_new[None, :]
    update = gradient * lax.rsqrt(second)
    spread = jnp.sqrt(jnp.mean(update * update))
    update = update / jnp.maximum(1.0, spread / 0.01)
    weight_new = (weight_f - update).astype(jnp.bfloat16)
    return (back, weight_new, row_new, col_new)

def reference(out_grad, routes, pre_act, out_weight, row_factor, col_factor):
    blocks = N_DP * N_EXPERT
    slots = slot_of(routes)
    dy_blocks = out_grad.reshape(blocks, TOK_DEV, D)
    outgoing = jnp.zeros((blocks, R, D), jnp.bfloat16)
    outgoing = outgoing.at[jnp.arange(blocks)[:, None], slots].set(dy_blocks)
    arrived = outgoing.reshape(N_DP, N_EXPERT, N_EXPERT, SLOT, D).transpose(2, 0, 1, 3, 4)
    arrived = arrived.reshape(N_EXPERT, N_DP * R, D)
    pre_rows = pre_act.reshape(N_DP, N_EXPERT, R, FF).transpose(1, 0, 2, 3).reshape(N_EXPERT, N_DP * R, FF)
    back, weight_new, row_new, col_new = lax.map(expert_step, (arrived, pre_rows, out_weight, row_factor, col_factor))
    returned = back.reshape(N_EXPERT, N_DP, N_EXPERT, SLOT, FF).transpose(1, 2, 0, 3, 4).reshape(blocks, R, FF)
    hidden_grad = jnp.take_along_axis(returned, slots[:, :, None], axis=1)
    return (hidden_grad.reshape(TOKENS, FF), weight_new, row_new, col_new)
```

```python
import functools
import jax
import jax.numpy as jnp
import numpy as np
from jax import lax
from jax.experimental import pallas as pl
from jax.experimental.pallas import tpu as pltpu
from jax.sharding import PartitionSpec as P

MESH = pl.DeviceIdType.MESH
F32, BF16 = jnp.float32, jnp.bfloat16


def up128(n):
    return -(-n // 128) * 128


def dot(a, b, ca=1, cb=0):
    return lax.dot_general(a, b, (((ca,), (cb,)), ((), ())), preferred_element_type=F32)


def onehot(hit):
    return jnp.where(hit, 1.0, 0.0).astype(BF16)


def kernel(cfg, og, rcol, rrow, pre, w, rf, cf, qn, qt,
           hid, neww, newrow, newcol,
           dy_out, dy_all, dyn, pre_all, wv, grad, snd, ret, colst, place, rfcol, rncol,
           loc, outs, dy_s, dy_r, fw_s, fw_r, pre_s, pre_r, rt_s, rt_r, st_s, st_r):
    n_dp, n_e, slot, groups, chunk = cfg
    tok, d = og.shape
    ff = wv.shape[0]
    r = pre.shape[0]
    packed = slot > 8
    half, dp_off, h0 = ff // 2, up128(d), d // 2 // 128 * 128
    hw = d - h0
    g = n_e // groups
    i, e = lax.axis_index("dp"), lax.axis_index("expert")
    total = n_dp * n_e
    flat = i * n_e + e
    others = [lax.rem(i + o, n_dp) for o in range(1, n_dp)]

    barrier = pltpu.get_barrier_semaphore()

    def greet(k, _):
        t = lax.rem(flat + k, total)
        ti = lax.div(t, n_e)
        pl.semaphore_signal(barrier, inc=1, device_id=(ti, t - ti * n_e), device_id_type=MESH)
        return 0

    lax.fori_loop(1, total, greet, 0)

    get_w = pltpu.make_async_copy(w.at[0], wv, loc.at[0])
    cols = lambda t: pl.ds(pl.multiple_of(t * ff, 128), ff)
    get_pre = pltpu.make_async_copy(pre.at[:, cols(i)], pre_all.at[i], loc.at[1])
    get_w.start()
    get_pre.start()

    same = rcol[...] == rrow[...]
    at_row = lax.broadcasted_iota(jnp.int32, (tok, tok), 0)
    at_col = lax.broadcasted_iota(jnp.int32, (tok, tok), 1)
    order = jnp.sum(jnp.where(same & (at_row < at_col), 1.0, 0.0), axis=0, keepdims=True)
    base = rrow[...].astype(F32) * 8.0 + order
    rows = lax.broadcasted_iota(jnp.int32, (n_e * 8, tok), 0).astype(F32)
    place[0] = onehot(rows == jnp.where(order < 8.0, base, -1.0))
    dy_out[:, :, 0:d] = dot(place[0], og[...]).reshape(n_e, 8, d).astype(BF16)
    if packed:
        place[1] = onehot(rows == jnp.where(order >= 8.0, base - 8.0, -1.0))
        place[2] = onehot(rows == jnp.where(order >= 8.0, base - 4.0, -1.0))
        tail = dot(place[1], og[:, 0:hw]) + dot(place[2], og[:, h0:d])
        dy_out[:, :, dp_off:dp_off + hw] = tail.reshape(n_e, 8, hw).astype(BF16)

    def peer(k):
        return lax.rem(e + lax.rem(k + n_e // 2 - 1, n_e - 1) + 1, n_e)

    def send_dy(k):
        t = peer(k)
        return pltpu.make_async_remote_copy(
            src_ref=dy_out.at[t], dst_ref=dy_all.at[i, e], send_sem=dy_s.at[t],
            recv_sem=dy_r.at[e], device_id=(i, t), device_id_type=MESH)

    def send_pre(t):
        return pltpu.make_async_remote_copy(
            src_ref=pre.at[:, cols(t)], dst_ref=pre_all.at[i], send_sem=pre_s.at[t],
            recv_sem=pre_r.at[i], device_id=(t, e), device_id_type=MESH)

    def send_fw(t, q):
        part = pl.ds(q * g, g)
        return pltpu.make_async_remote_copy(
            src_ref=dy_all.at[i, part], dst_ref=dy_all.at[i, part], send_sem=fw_s.at[t, q],
            recv_sem=fw_r.at[i, q], device_id=(t, e), device_id_type=MESH)

    def send_ret(t, j):
        return pltpu.make_async_remote_copy(
            src_ref=snd.at[t, j], dst_ref=ret.at[i, e], send_sem=rt_s.at[t, j],
            recv_sem=rt_r.at[i, e], device_id=(t, j), device_id_type=MESH)

    def send_st(t):
        return pltpu.make_async_remote_copy(
            src_ref=colst.at[i], dst_ref=colst.at[i], send_sem=st_s.at[t],
            recv_sem=st_r.at[i], device_id=(t, e), device_id_type=MESH)

    def loop(n, act):
        def step(k, _):
            act(k)
            return 0
        lax.fori_loop(0, n, step, 0)

    pl.semaphore_wait(barrier, total - 1)
    loop(n_e - 1, lambda k: send_dy(k).start())
    own = pltpu.make_async_copy(dy_out.at[e], dy_all.at[i, e], dy_r.at[e])
    own.start()
    for t in others:
        send_pre(t).start()

    for b in range(ff // 128):
        lane = slice(b * 128, b * 128 + 128)
        rfcol[lane, :] = jnp.broadcast_to(rf[0:1, lane], (128, 128)).T

    for k in range(groups):
        q = lax.rem(lax.div(e, g) + k, groups)
        for m in range(g):
            j = q * g + m
            pltpu.make_async_copy(dy_out.at[0], dy_all.at[i, j], dy_r.at[j]).wait()
        for t in others:
            send_fw(t, q).start()

    def flat_rows(x):
        return x.astype(F32).reshape(x.shape[0] * 8, x.shape[2]).astype(BF16)

    def back(t):
        dy = dot(qn[0], flat_rows(dy_all[t, :, :, 0:d]))
        if packed:
            tail = flat_rows(dy_all[t, :, :, dp_off:dp_off + hw])
            dy = dy + jnp.concatenate([dot(qn[1], tail[:, 0:h0]), dot(qn[2], tail)], axis=1)
        dy = dy.astype(BF16)
        dyn[t] = dy
        tail = None
        for c in range(2 if packed else 1):
            wide = half if packed else ff
            span = slice(c * wide, c * wide + wide)
            bk = dot(dy, wv[span, :], 1, 1)
            keep = pre_all[t, :, span].astype(F32) > 0.0
            bk = jnp.where(keep, bk, 0.0).astype(BF16)
            snd[t, :, :, span] = dot(qt[0], bk).reshape(n_e, 8, wide).astype(BF16)
            if packed:
                part = dot(qt[1 + c], bk)
                tail = part if tail is None else tail + part
        if packed:
            snd[t, :, :, ff:ff + half] = tail.reshape(n_e, 8, half).astype(BF16)

    get_w.wait()
    get_pre.wait()
    back(i)
    loop(n_e - 1, lambda k: send_ret(i, peer(k)).start())
    own_ret = pltpu.make_async_copy(snd.at[i, e], ret.at[i, e], rt_r.at[i, e])
    own_ret.start()

    for t in others:
        for q in range(groups):
            part = pl.ds(q * g, g)
            pltpu.make_async_copy(dy_all.at[i, part], dy_all.at[t, part], fw_r.at[t, q]).wait()
        pltpu.make_async_copy(pre_all.at[i], pre_all.at[t], pre_r.at[t]).wait()
        back(t)
        loop(n_e, lambda k: send_ret(t, lax.rem(e + n_e // 2 + k, n_e)).start())

    def gradient(c, carry):
        col, weighted = carry
        span = pl.ds(pl.multiple_of(c * chunk, 128), chunk)
        acc = None
        for t in range(n_dp):
            hidden = jnp.maximum(pre_all[t, :, span], 0)
            part = dot(hidden, dyn[t], 0, 0)
            acc = part if acc is None else acc + part
        grad[span, :] = acc
        sq = acc * acc
        rn = 0.8 * rfcol[span, 0:1] + 0.2 * (jnp.sum(sq, axis=1, keepdims=True) / d + 1e-30)
        rncol[span, :] = jnp.broadcast_to(rn, (chunk, 128))
        return (col + jnp.sum(sq, axis=0, keepdims=True),
                weighted + jnp.sum(sq * (1.0 / rn), axis=0, keepdims=True))

    zero = jnp.zeros((1, d), F32)
    col, weighted = lax.fori_loop(0, ff // chunk, gradient, (zero, zero))
    colst[i, 0:1, :] = col
    colst[i, 1:2, :] = weighted
    for t in others:
        send_st(t).start()
    for b in range(ff // 128):
        lane = slice(b * 128, b * 128 + 128)
        newrow[0:1, lane] = rncol[lane, :].T[0:1, :]
    for t in others:
        pltpu.make_async_copy(colst.at[i], colst.at[t], st_r.at[t]).wait()
    col, weighted = zero, zero
    for t in range(n_dp):
        col = col + colst[t, 0:1, :]
        weighted = weighted + colst[t, 1:2, :]
    full = ff * n_dp
    cn = 0.8 * cf[...] + 0.2 * (col / full + 1e-30)
    newcol[...] = cn
    spread = jnp.sqrt(jnp.sum(weighted / cn, axis=1, keepdims=True) / (full * d))
    cs = lax.rsqrt(cn) / jnp.maximum(1.0, spread / 0.01)

    def write(c):
        span = pl.ds(pl.multiple_of(c * chunk, 128), chunk)
        return pltpu.make_async_copy(wv.at[span, :], neww.at[0, span, :], outs.at[c])

    def apply(c):
        span = pl.ds(pl.multiple_of(c * chunk, 128), chunk)
        update = grad[span, :] * lax.rsqrt(rncol[span, 0:1]) * cs
        wv[span, :] = (wv[span, :].astype(F32) - update).astype(BF16)
        write(c).start()

    loop(ff // chunk, apply)

    for t in [i] + others:
        loop(n_e, lambda j: pltpu.make_async_copy(
            snd.at[0, 0], ret.at[t, j], rt_r.at[t, j]).wait())
        for c in range(2 if packed else 1):
            wide = half if packed else ff
            got = dot(place[0], flat_rows(ret[t, :, :, c * wide:c * wide + wide]), 0, 0)
            if packed:
                got = got + dot(place[1 + c], flat_rows(ret[t, :, :, ff:ff + half]), 0, 0)
            hid[:, pl.ds(pl.multiple_of(t * ff + c * wide, 128), wide)] = got.astype(BF16)

    loop(n_e - 1, lambda k: send_dy(k).wait_send())
    loop(n_e - 1, lambda k: send_ret(i, peer(k)).wait_send())
    for t in others:
        send_pre(t).wait_send()
        for q in range(groups):
            send_fw(t, q).wait_send()
        loop(n_e, lambda k: send_ret(t, k).wait_send())
        send_st(t).wait_send()
    loop(ff // chunk, lambda c: write(c).wait())


def shards(out_grad, routes, pre_act, out_weight, row_factor, col_factor):
    n_dp, n_e = lax.axis_size("dp"), lax.axis_size("expert")
    tok, d = out_grad.shape
    r = pre_act.shape[0]
    ff = out_weight.shape[1]
    slot = r // n_e
    packed = slot > 8
    assert slot <= 12
    kinds = 3 if packed else 1
    groups = 4
    chunk = next(c for c in (384, 256, 128) if ff % c == 0)
    wide_d = up128(d) + d - d // 2 // 128 * 128 if packed else d
    wide_f = ff + ff // 2 if packed else ff
    row = np.arange(r)
    src, s = row // slot, row % slot
    q = np.zeros((kinds, r, n_e * 8), np.float32)
    low = s < 8
    q[0, row[low], (src * 8 + s)[low]] = 1
    if packed:
        q[1, row[~low], (src * 8 + s - 8)[~low]] = 1
        q[2, row[~low], (src * 8 + s - 4)[~low]] = 1
    qn = jnp.asarray(q, BF16)
    qt = jnp.asarray(q.transpose(0, 2, 1), BF16)
    vm = pl.BlockSpec(memory_space=pltpu.VMEM)
    hbm = pl.BlockSpec(memory_space=pl.ANY)
    dma = pltpu.SemaphoreType.DMA
    sds = jax.ShapeDtypeStruct
    return pl.pallas_call(
        functools.partial(kernel, (n_dp, n_e, slot, groups, chunk)),
        out_shape=(sds((tok, ff * n_dp), BF16), sds((1, ff, d), BF16),
                   sds((1, ff), F32), sds((1, d), F32)),
        in_specs=[vm, vm, vm, hbm, hbm, vm, vm, vm, vm],
        out_specs=(vm, hbm, vm, vm),
        scratch_shapes=[
            pltpu.VMEM((n_e, 8, wide_d), BF16),
            pltpu.VMEM((n_dp, n_e, 8, wide_d), BF16),
            pltpu.VMEM((n_dp, r, d), BF16),
            pltpu.VMEM((n_dp, r, ff), BF16),
            pltpu.VMEM((ff, d), BF16),
            pltpu.VMEM((ff, d), F32),
            pltpu.VMEM((n_dp, n_e, 8, wide_f), BF16),
            pltpu.VMEM((n_dp, n_e, 8, wide_f), BF16),
            pltpu.VMEM((n_dp, 2, d), F32),
            pltpu.VMEM((kinds, n_e * 8, tok), BF16),
            pltpu.VMEM((ff, 128), F32),
            pltpu.VMEM((ff, 128), F32),
            dma((2,)), dma((ff // chunk,)), dma((n_e,)), dma((n_e,)),
            dma((n_dp, groups)), dma((n_dp, groups)), dma((n_dp,)), dma((n_dp,)),
            dma((n_dp, n_e)), dma((n_dp, n_e)), dma((n_dp,)), dma((n_dp,)),
        ],
        compiler_params=pltpu.CompilerParams(
            collective_id=0, has_side_effects=True, vmem_limit_bytes=60 * 1024 * 1024),
    )(out_grad, routes, routes.reshape(1, tok), pre_act, out_weight, row_factor, col_factor, qn, qt)


def solution(mesh):
    placed = (
        P(("dp", "expert"), None),
        P(("dp", "expert"), None),
        P(("dp", "expert"), None),
        P("expert", "dp", None),
        P("expert", "dp"),
        P("expert", None),
    )
    return jax.shard_map(
        shards,
        mesh=mesh,
        in_specs=placed,
        out_specs=(
            P(("dp", "expert"), None),
            P("expert", "dp", None),
            P("expert", "dp"),
            P("expert", None),
        ),
        check_vma=False,
    )
```

```python
import functools
import jax
import jax.numpy as jnp
import numpy as np
from jax import lax
from jax.experimental import pallas as pl
from jax.experimental.pallas import tpu as pltpu
from jax.sharding import PartitionSpec as P

MESH = pl.DeviceIdType.MESH
F32, BF16 = jnp.float32, jnp.bfloat16


def up128(n):
    return -(-n // 128) * 128


def dot(a, b, ca=1, cb=0):
    return lax.dot_general(a, b, (((ca,), (cb,)), ((), ())), preferred_element_type=F32)


def onehot(hit):
    return jnp.where(hit, 1.0, 0.0).astype(BF16)


def kernel(cfg, og, rrow, pre, w, rf, cf, qn, qt,
           hid, neww, newrow, newcol,
           dy_out, dy_all, dyn, pre_all, wv, grad, snd, ret, colst, place, colacc, cspad, cscol,
           loc, dy_s, dy_r, fw_s, fw_r, pre_s, pre_r, rt_s, rt_r, st_s, st_r):
    n_dp, n_e, slot, groups, chunk, deep = cfg
    d, tok = og.shape
    ff = wv.shape[1]
    r = pre.shape[0]
    packed = slot > 8
    half, dp_off, h0 = ff // 2, up128(d), d // 2 // 128 * 128
    hw = d - h0
    g = n_e // groups
    i, e = lax.axis_index("dp"), lax.axis_index("expert")
    total = n_dp * n_e
    flat = i * n_e + e
    others = [lax.rem(i + o, n_dp) for o in range(1, n_dp)]

    barrier = pltpu.get_barrier_semaphore()

    def greet(k, _):
        t = lax.rem(flat + k, total)
        ti = lax.div(t, n_e)
        pl.semaphore_signal(barrier, inc=1, device_id=(ti, t - ti * n_e), device_id_type=MESH)
        return 0

    lax.fori_loop(1, total, greet, 0)

    get_w = pltpu.make_async_copy(w.at[0], wv, loc.at[0])
    cols = lambda t: pl.ds(pl.multiple_of(t * ff, 128), ff)
    get_pre = pltpu.make_async_copy(pre.at[:, cols(i)], pre_all.at[i], loc.at[1])
    get_w.start()
    get_pre.start()

    named = jnp.broadcast_to(rrow[...].astype(F32), (tok, tok))
    same = named == named.T
    at_row = lax.broadcasted_iota(jnp.int32, (tok, tok), 0)
    at_col = lax.broadcasted_iota(jnp.int32, (tok, tok), 1)
    order = jnp.sum(jnp.where(same & (at_row < at_col), 1.0, 0.0), axis=0, keepdims=True)
    base = rrow[...].astype(F32) * 8.0 + order
    rows = lax.broadcasted_iota(jnp.int32, (n_e * 8, tok), 0).astype(F32)
    place[0] = onehot(rows == jnp.where(order < 8.0, base, -1.0))
    dy_out[:, :, 0:d] = dot(place[0], og[...], 1, 1).reshape(n_e, 8, d).astype(BF16)
    if packed:
        place[1] = onehot(rows == jnp.where(order >= 8.0, base - 8.0, -1.0))
        place[2] = onehot(rows == jnp.where(order >= 8.0, base - 4.0, -1.0))
        tail = dot(place[1], og[0:hw, :], 1, 1) + dot(place[2], og[h0:d, :], 1, 1)
        dy_out[:, :, dp_off:dp_off + hw] = tail.reshape(n_e, 8, hw).astype(BF16)

    def peer(k):
        return lax.rem(e + lax.rem(k + n_e // 2 - 1, n_e - 1) + 1, n_e)

    def send_dy(k):
        t = peer(k)
        return pltpu.make_async_remote_copy(
            src_ref=dy_out.at[t], dst_ref=dy_all.at[i, e], send_sem=dy_s.at[t],
            recv_sem=dy_r.at[e], device_id=(i, t), device_id_type=MESH)

    def send_pre(t):
        return pltpu.make_async_remote_copy(
            src_ref=pre.at[:, cols(t)], dst_ref=pre_all.at[i], send_sem=pre_s.at[t],
            recv_sem=pre_r.at[i], device_id=(t, e), device_id_type=MESH)

    def send_fw(t, q):
        part = pl.ds(q * g, g)
        return pltpu.make_async_remote_copy(
            src_ref=dy_all.at[i, part], dst_ref=dy_all.at[i, part], send_sem=fw_s.at[t, q],
            recv_sem=fw_r.at[i, q], device_id=(t, e), device_id_type=MESH)

    def send_ret(t, j):
        return pltpu.make_async_remote_copy(
            src_ref=snd.at[t, j], dst_ref=ret.at[i, e], send_sem=rt_s.at[t, j],
            recv_sem=rt_r.at[i, e], device_id=(t, j), device_id_type=MESH)

    def send_st(t):
        return pltpu.make_async_remote_copy(
            src_ref=colst.at[i], dst_ref=colst.at[i], send_sem=st_s.at[t],
            recv_sem=st_r.at[i], device_id=(t, e), device_id_type=MESH)

    def loop(n, act):
        def step(k, _):
            act(k)
            return 0
        lax.fori_loop(0, n, step, 0)

    pl.semaphore_wait(barrier, total - 1)
    loop(n_e - 1, lambda k: send_dy(k).start())
    own = pltpu.make_async_copy(dy_out.at[e], dy_all.at[i, e], dy_r.at[e])
    own.start()
    for t in others:
        send_pre(t).start()

    colacc[...] = jnp.zeros_like(colacc)

    for k in range(groups):
        q = lax.rem(lax.div(e, g) + k, groups)
        for m in range(g):
            j = q * g + m
            pltpu.make_async_copy(dy_out.at[0], dy_all.at[i, j], dy_r.at[j]).wait()
        for t in others:
            send_fw(t, q).start()

    def flat_rows(x):
        return x.astype(F32).reshape(x.shape[0] * 8, x.shape[2]).astype(BF16)

    def back(t):
        dy = dot(qn[0], flat_rows(dy_all[t, :, :, 0:d]))
        if packed:
            tail = flat_rows(dy_all[t, :, :, dp_off:dp_off + hw])
            dy = dy + jnp.concatenate([dot(qn[1], tail[:, 0:h0]), dot(qn[2], tail)], axis=1)
        dy = dy.astype(BF16)
        dyn[t] = dy
        tail = None
        for c in range(2 if packed else 1):
            wide = half if packed else ff
            span = slice(c * wide, c * wide + wide)
            bk = dot(dy, wv[:, span])
            keep = pre_all[t, :, span].astype(F32) > 0.0
            bk = jnp.where(keep, bk, 0.0).astype(BF16)
            snd[t, :, :, span] = dot(qt[0], bk).reshape(n_e, 8, wide).astype(BF16)
            if packed:
                part = dot(qt[1 + c], bk)
                tail = part if tail is None else tail + part
        if packed:
            snd[t, :, :, ff:ff + half] = tail.reshape(n_e, 8, half).astype(BF16)

    get_w.wait()
    get_pre.wait()
    back(i)
    loop(n_e - 1, lambda k: send_ret(i, peer(k)).start())
    own_ret = pltpu.make_async_copy(snd.at[i, e], ret.at[i, e], rt_r.at[i, e])
    own_ret.start()

    for t in others:
        for q in range(groups):
            part = pl.ds(q * g, g)
            pltpu.make_async_copy(dy_all.at[i, part], dy_all.at[t, part], fw_r.at[t, q]).wait()
        pltpu.make_async_copy(pre_all.at[i], pre_all.at[t], pre_r.at[t]).wait()
        back(t)
        loop(n_e, lambda k: send_ret(t, lax.rem(e + n_e // 2 + k, n_e)).start())

    def gradient(c):
        span = pl.ds(pl.multiple_of(c * chunk, 128), chunk)
        acc = None
        for t in range(n_dp):
            part = dot(dyn[t], jnp.maximum(pre_all[t, :, span], 0), 0, 0)
            acc = part if acc is None else acc + part
        grad[:, span] = acc
        sq = acc * acc
        rn = 0.8 * rf[0:1, span] + 0.2 * (jnp.sum(sq, axis=0, keepdims=True) / d + 1e-30)
        newrow[0:1, span] = rn
        for k, x in enumerate((sq, sq * (1.0 / rn))):
            folded = x[:, 0:128]
            for b in range(1, chunk // 128):
                folded = folded + x[:, b * 128:b * 128 + 128]
            colacc[k, 0:d, :] += folded

    loop(ff // chunk, gradient)
    blocks = [(b, min(b + 128, d)) for b in range(0, d, 128)]
    for k in range(2):
        for lo, hi in blocks:
            sums = jnp.sum(colacc[k, lo:lo + 128, :].T, axis=0, keepdims=True)
            colst[i, k:k + 1, lo:hi] = sums[:, 0:hi - lo]
    for t in others:
        send_st(t).start()
    for t in others:
        pltpu.make_async_copy(colst.at[i], colst.at[t], st_r.at[t]).wait()
    col, weighted = jnp.zeros((1, d), F32), jnp.zeros((1, d), F32)
    for t in range(n_dp):
        col = col + colst[t, 0:1, :]
        weighted = weighted + colst[t, 1:2, :]
    full = ff * n_dp
    cn = 0.8 * cf[...] + 0.2 * (col / full + 1e-30)
    newcol[...] = cn
    spread = jnp.sqrt(jnp.sum(weighted / cn, axis=1, keepdims=True) / (full * d))
    cspad[...] = jnp.zeros_like(cspad)
    cspad[0:1, 0:d] = lax.rsqrt(cn) / jnp.maximum(1.0, spread / 0.01)
    for lo, hi in blocks:
        cscol[lo:lo + 128, :] = jnp.broadcast_to(cspad[0:1, lo:lo + 128], (128, 128)).T

    def apply(c):
        span = pl.ds(pl.multiple_of(c * deep, 16), deep)
        update = grad[span, :] * lax.rsqrt(newrow[...]) * cscol[span, 0:1]
        neww[0, span, :] = (wv[span, :].astype(F32) - update).astype(BF16)

    loop(d // deep, apply)

    for t in [i] + others:
        loop(n_e, lambda j: pltpu.make_async_copy(
            snd.at[0, 0], ret.at[t, j], rt_r.at[t, j]).wait())
        for c in range(2 if packed else 1):
            wide = half if packed else ff
            got = dot(place[0], flat_rows(ret[t, :, :, c * wide:c * wide + wide]), 0, 0)
            if packed:
                got = got + dot(place[1 + c], flat_rows(ret[t, :, :, ff:ff + half]), 0, 0)
            hid[:, pl.ds(pl.multiple_of(t * ff + c * wide, 128), wide)] = got.astype(BF16)

    loop(n_e - 1, lambda k: send_dy(k).wait_send())
    loop(n_e - 1, lambda k: send_ret(i, peer(k)).wait_send())
    for t in others:
        send_pre(t).wait_send()
        for q in range(groups):
            send_fw(t, q).wait_send()
        loop(n_e, lambda k: send_ret(t, k).wait_send())
        send_st(t).wait_send()


def flush(a, b, c, d, ao, bo, co, do, sem):
    pairs = ((b, bo), (a, ao), (c, co), (d, do))
    copies = [pltpu.make_async_copy(x, y, sem.at[k]) for k, (x, y) in enumerate(pairs)]
    for copy in copies:
        copy.start()
    for copy in copies:
        copy.wait()


def shards(out_grad, routes, pre_act, out_weight, row_factor, col_factor):
    n_dp, n_e = lax.axis_size("dp"), lax.axis_size("expert")
    tok, d = out_grad.shape
    r = pre_act.shape[0]
    ff = out_weight.shape[1]
    slot = r // n_e
    packed = slot > 8
    assert slot <= 12
    kinds = 3 if packed else 1
    groups = 4
    chunk = next(c for c in (384, 256, 128) if ff % c == 0)
    deep = max(c for c in range(16, 257, 16) if d % c == 0)
    wide_d = up128(d) + d - d // 2 // 128 * 128 if packed else d
    wide_f = ff + ff // 2 if packed else ff
    row = np.arange(r)
    src, s = row // slot, row % slot
    q = np.zeros((kinds, r, n_e * 8), np.float32)
    low = s < 8
    q[0, row[low], (src * 8 + s)[low]] = 1
    if packed:
        q[1, row[~low], (src * 8 + s - 8)[~low]] = 1
        q[2, row[~low], (src * 8 + s - 4)[~low]] = 1
    qn = jnp.asarray(q, BF16)
    qt = jnp.asarray(q.transpose(0, 2, 1), BF16)
    vm = pl.BlockSpec(memory_space=pltpu.VMEM)
    hbm = pl.BlockSpec(memory_space=pl.ANY)
    dma = pltpu.SemaphoreType.DMA
    out = pltpu.VMEM
    hid, neww, newrow, newcol = pl.pallas_call(
        functools.partial(kernel, (n_dp, n_e, slot, groups, chunk, deep)),
        out_shape=(out((tok, ff * n_dp), BF16), out((1, d, ff), BF16),
                   out((1, ff), F32), out((1, d), F32)),
        in_specs=[vm, vm, hbm, hbm, vm, vm, vm, vm],
        out_specs=(vm, vm, vm, vm),
        scratch_shapes=[
            pltpu.VMEM((n_e, 8, wide_d), BF16),
            pltpu.VMEM((n_dp, n_e, 8, wide_d), BF16),
            pltpu.VMEM((n_dp, r, d), BF16),
            pltpu.VMEM((n_dp, r, ff), BF16),
            pltpu.VMEM((d, ff), BF16),
            pltpu.VMEM((d, ff), F32),
            pltpu.VMEM((n_dp, n_e, 8, wide_f), BF16),
            pltpu.VMEM((n_dp, n_e, 8, wide_f), BF16),
            pltpu.VMEM((n_dp, 2, d), F32),
            pltpu.VMEM((kinds, n_e * 8, tok), BF16),
            pltpu.VMEM((2, up128(d), 128), F32),
            pltpu.VMEM((1, up128(d)), F32),
            pltpu.VMEM((up128(d), 128), F32),
            dma((2,)), dma((n_e,)), dma((n_e,)),
            dma((n_dp, groups)), dma((n_dp, groups)), dma((n_dp,)), dma((n_dp,)),
            dma((n_dp, n_e)), dma((n_dp, n_e)), dma((n_dp,)), dma((n_dp,)),
        ],
        compiler_params=pltpu.CompilerParams(
            collective_id=0, has_side_effects=True, vmem_limit_bytes=59 * 1024 * 1024),
    )(out_grad.T, routes.reshape(1, tok), pre_act, jnp.swapaxes(out_weight, 1, 2), row_factor,
      col_factor, qn, qt)
    held = (hid, neww, newrow, newcol)
    hid, neww, newrow, newcol = pl.pallas_call(
        flush,
        out_shape=tuple(jax.ShapeDtypeStruct(x.shape, x.dtype) for x in held),
        in_specs=[vm] * 4,
        out_specs=[hbm] * 4,
        scratch_shapes=[dma((4,))],
        compiler_params=pltpu.CompilerParams(vmem_limit_bytes=1024 * 1024),
    )(*held)
    return hid, jnp.swapaxes(neww, 1, 2), newrow, newcol


def solution(mesh):
    placed = (
        P(("dp", "expert"), None),
        P(("dp", "expert"), None),
        P(("dp", "expert"), None),
        P("expert", "dp", None),
        P("expert", "dp"),
        P("expert", None),
    )
    return jax.shard_map(
        shards,
        mesh=mesh,
        in_specs=placed,
        out_specs=(
            P(("dp", "expert"), None),
            P("expert", "dp", None),
            P("expert", "dp"),
            P("expert", None),
        ),
        check_vma=False,
    )
```

```python
import functools
import jax
import jax.numpy as jnp
import numpy as np
from jax import lax
from jax.experimental import pallas as pl
from jax.experimental.pallas import tpu as pltpu
from jax.sharding import PartitionSpec as P

MESH = pl.DeviceIdType.MESH
F32, BF16 = jnp.float32, jnp.bfloat16


def up128(n):
    return -(-n // 128) * 128


def dot(a, b, ca=1, cb=0):
    return lax.dot_general(a, b, (((ca,), (cb,)), ((), ())), preferred_element_type=F32)


def onehot(hit):
    return jnp.where(hit, 1.0, 0.0).astype(BF16)


def kernel(cfg, og, rrow, pre, w, rf, cf, qn, qt,
           hid, neww, newrow, newcol,
           dy_out, dy_all, dyn, pre_all, wv, grad, snd, ret, colst, place, colacc, cspad, cscol,
           loc, dy_s, dy_r, fw_s, fw_r, pre_s, pre_r, rt_s, rt_r, st_s, st_r):
    n_dp, n_e, slot, groups, chunk, deep = cfg
    d, tok = og.shape
    ff = wv.shape[1]
    r = pre.shape[0]
    packed = slot > 8
    half, dp_off, h0 = ff // 2, up128(d), d // 2 // 128 * 128
    rest = d - 2 * h0
    g = n_e // groups
    i, e = lax.axis_index("dp"), lax.axis_index("expert")
    total = n_dp * n_e
    flat = i * n_e + e
    others = [lax.rem(i + o, n_dp) for o in range(1, n_dp)]

    barrier = pltpu.get_barrier_semaphore()

    def greet(k, _):
        t = lax.rem(flat + k, total)
        ti = lax.div(t, n_e)
        pl.semaphore_signal(barrier, inc=1, device_id=(ti, t - ti * n_e), device_id_type=MESH)
        return 0

    lax.fori_loop(1, total, greet, 0)

    get_w = pltpu.make_async_copy(w.at[0], wv, loc.at[0])
    cols = lambda t: pl.ds(pl.multiple_of(t * ff, 128), ff)
    get_pre = pltpu.make_async_copy(pre.at[:, cols(i)], pre_all.at[i], loc.at[1])
    get_w.start()
    get_pre.start()

    named = jnp.broadcast_to(rrow[...].astype(F32), (tok, tok))
    same = named == named.T
    at_row = lax.broadcasted_iota(jnp.int32, (tok, tok), 0)
    at_col = lax.broadcasted_iota(jnp.int32, (tok, tok), 1)
    order = jnp.sum(jnp.where(same & (at_row < at_col), 1.0, 0.0), axis=0, keepdims=True)
    base = rrow[...].astype(F32) * 8.0 + order
    rows = lax.broadcasted_iota(jnp.int32, (n_e * 8, tok), 0).astype(F32)
    place[0] = onehot(rows == jnp.where(order < 8.0, base, -1.0))
    dy_out[:, :, 0:d] = dot(place[0], og[...], 1, 1).reshape(n_e, 8, d).astype(BF16)
    if packed:
        place[1] = onehot(rows == jnp.where(order >= 8.0, base - 8.0, -1.0))
        place[2] = onehot(rows == jnp.where(order >= 8.0, base - 4.0, -1.0))
        tail = dot(place[1], og[0:h0, :], 1, 1) + dot(place[2], og[h0:2 * h0, :], 1, 1)
        dy_out[:, :, dp_off:dp_off + h0] = tail.reshape(n_e, 8, h0).astype(BF16)
        if rest:
            more = dot(place[1], og[2 * h0:d, :], 1, 1)
            dy_out[:, :, d:d + rest] = more.reshape(n_e, 8, rest).astype(BF16)

    def peer(k):
        return lax.rem(e + lax.rem(k + n_e // 2 - 1, n_e - 1) + 1, n_e)

    def send_dy(k):
        t = peer(k)
        return pltpu.make_async_remote_copy(
            src_ref=dy_out.at[t], dst_ref=dy_all.at[i, e], send_sem=dy_s.at[t],
            recv_sem=dy_r.at[e], device_id=(i, t), device_id_type=MESH)

    def send_pre(t):
        return pltpu.make_async_remote_copy(
            src_ref=pre.at[:, cols(t)], dst_ref=pre_all.at[i], send_sem=pre_s.at[t],
            recv_sem=pre_r.at[i], device_id=(t, e), device_id_type=MESH)

    def send_fw(t, q):
        part = pl.ds(q * g, g)
        return pltpu.make_async_remote_copy(
            src_ref=dy_all.at[i, part], dst_ref=dy_all.at[i, part], send_sem=fw_s.at[t, q],
            recv_sem=fw_r.at[i, q], device_id=(t, e), device_id_type=MESH)

    def send_ret(t, j):
        return pltpu.make_async_remote_copy(
            src_ref=snd.at[t, j], dst_ref=ret.at[i, e], send_sem=rt_s.at[t, j],
            recv_sem=rt_r.at[i, e], device_id=(t, j), device_id_type=MESH)

    def send_st(t):
        return pltpu.make_async_remote_copy(
            src_ref=colst.at[i], dst_ref=colst.at[i], send_sem=st_s.at[t],
            recv_sem=st_r.at[i], device_id=(t, e), device_id_type=MESH)

    near = lax.div(e, n_e // 2)
    far = 1 - near

    def loop(n, act):
        def step(k, _):
            act(k)
            return 0
        lax.fori_loop(0, n, step, 0)

    pl.semaphore_wait(barrier, total - 1)
    for t in others:
        send_pre(t).start()
    loop(n_e - 1, lambda k: send_dy(k).start())
    own = pltpu.make_async_copy(dy_out.at[e], dy_all.at[i, e], dy_r.at[e])
    own.start()

    colacc[...] = jnp.zeros_like(colacc)

    for k in range(groups):
        q = lax.rem(far * (groups // 2) + k, groups)
        for m in range(g):
            j = q * g + m
            pltpu.make_async_copy(dy_out.at[0], dy_all.at[i, j], dy_r.at[j]).wait()
        for t in others:
            send_fw(t, q).start()

    def flat_rows(x):
        return x.astype(F32).reshape(x.shape[0] * 8, x.shape[2]).astype(BF16)

    def back(t, first, count):
        n = count * slot
        part = pl.ds(first, count)
        where = pl.ds(first * slot if isinstance(first, int) else pl.multiple_of(first * slot, 16), n)
        dy = dot(qn[0, 0:n, 0:count * 8], flat_rows(dy_all[t, part, :, 0:d]))
        if packed:
            q_lo, q_hi = qn[1, 0:n, 0:count * 8], qn[2, 0:n, 0:count * 8]
            tail = flat_rows(dy_all[t, part, :, dp_off:dp_off + h0])
            pieces = [dot(q_lo, tail), dot(q_hi, tail)]
            if rest:
                ends = dot(q_lo, flat_rows(dy_all[t, part, :, 2 * h0:dp_off]))
                pieces.append(ends[:, d - 2 * h0:d - 2 * h0 + rest])
            dy = dy + jnp.concatenate(pieces, axis=1)
        dy = dy.astype(BF16)
        dyn[t, where, :] = dy
        tail = None
        for c in range(2 if packed else 1):
            wide = half if packed else ff
            span = slice(c * wide, c * wide + wide)
            bk = dot(dy, wv[:, span])
            keep = pre_all[t, where, span].astype(F32) > 0.0
            bk = jnp.where(keep, bk, 0.0).astype(BF16)
            snd[t, part, :, span] = dot(qt[0, 0:count * 8, 0:n], bk).reshape(count, 8, wide).astype(BF16)
            if packed:
                more = dot(qt[1 + c, 0:count * 8, 0:n], bk)
                tail = more if tail is None else tail + more
        if packed:
            snd[t, part, :, ff:ff + half] = tail.reshape(count, 8, half).astype(BF16)

    get_w.wait()
    get_pre.wait()
    back(i, 0, n_e)
    loop(n_e - 1, lambda k: send_ret(i, peer(k)).start())
    own_ret = pltpu.make_async_copy(snd.at[i, e], ret.at[i, e], rt_r.at[i, e])
    own_ret.start()

    side = n_e // 2

    def send_side(t, which):
        loop(side, lambda k: send_ret(t, which * side + lax.rem(e + k, side)).start())

    for t in others:
        pltpu.make_async_copy(pre_all.at[i], pre_all.at[t], pre_r.at[t]).wait()
        for which in (far, near):
            for k in range(groups // 2):
                q = which * (groups // 2) + k
                part = pl.ds(q * g, g)
                pltpu.make_async_copy(dy_all.at[i, part], dy_all.at[t, part], fw_r.at[t, q]).wait()
            back(t, which * side, side)
            if which is far:
                send_side(t, far)

    def gradient(c):
        span = pl.ds(pl.multiple_of(c * chunk, 128), chunk)
        acc = None
        for t in range(n_dp):
            part = dot(dyn[t], jnp.maximum(pre_all[t, :, span], 0), 0, 0)
            acc = part if acc is None else acc + part
        grad[:, span] = acc
        sq = acc * acc
        rn = 0.8 * rf[0:1, span] + 0.2 * (jnp.sum(sq, axis=0, keepdims=True) / d + 1e-30)
        newrow[0:1, span] = rn
        for k, x in enumerate((sq, sq * (1.0 / rn))):
            folded = x[:, 0:128]
            for b in range(1, chunk // 128):
                folded = folded + x[:, b * 128:b * 128 + 128]
            colacc[k, 0:d, :] += folded

    loop(ff // chunk, gradient)
    blocks = [(b, min(b + 128, d)) for b in range(0, d, 128)]
    for k in range(2):
        for lo, hi in blocks:
            sums = jnp.sum(colacc[k, lo:lo + 128, :].T, axis=0, keepdims=True)
            colst[i, k:k + 1, lo:hi] = sums[:, 0:hi - lo]
    for t in others:
        send_st(t).start()
        send_side(t, near)
    for t in others:
        pltpu.make_async_copy(colst.at[i], colst.at[t], st_r.at[t]).wait()
    col, weighted = jnp.zeros((1, d), F32), jnp.zeros((1, d), F32)
    for t in range(n_dp):
        col = col + colst[t, 0:1, :]
        weighted = weighted + colst[t, 1:2, :]
    full = ff * n_dp
    cn = 0.8 * cf[...] + 0.2 * (col / full + 1e-30)
    newcol[...] = cn
    spread = jnp.sqrt(jnp.sum(weighted / cn, axis=1, keepdims=True) / (full * d))
    cspad[...] = jnp.zeros_like(cspad)
    cspad[0:1, 0:d] = lax.rsqrt(cn) / jnp.maximum(1.0, spread / 0.01)
    for lo, hi in blocks:
        cscol[lo:lo + 128, :] = jnp.broadcast_to(cspad[0:1, lo:lo + 128], (128, 128)).T

    def apply(c):
        span = pl.ds(pl.multiple_of(c * deep, 16), deep)
        update = grad[span, :] * lax.rsqrt(newrow[...]) * cscol[span, 0:1]
        neww[0, span, :] = (wv[span, :].astype(F32) - update).astype(BF16)

    loop(d // deep, apply)

    for t in [i] + others:
        loop(n_e, lambda j: pltpu.make_async_copy(
            snd.at[0, 0], ret.at[t, j], rt_r.at[t, j]).wait())
        for c in range(2 if packed else 1):
            wide = half if packed else ff
            got = dot(place[0], flat_rows(ret[t, :, :, c * wide:c * wide + wide]), 0, 0)
            if packed:
                got = got + dot(place[1 + c], flat_rows(ret[t, :, :, ff:ff + half]), 0, 0)
            hid[:, pl.ds(pl.multiple_of(t * ff + c * wide, 128), wide)] = got.astype(BF16)

    loop(n_e - 1, lambda k: send_dy(k).wait_send())
    loop(n_e - 1, lambda k: send_ret(i, peer(k)).wait_send())
    for t in others:
        send_pre(t).wait_send()
        for q in range(groups):
            send_fw(t, q).wait_send()
        loop(n_e, lambda k: send_ret(t, k).wait_send())
        send_st(t).wait_send()


def flush(a, b, c, d, ao, bo, co, do, sem):
    pairs = ((b, bo), (a, ao), (c, co), (d, do))
    copies = [pltpu.make_async_copy(x, y, sem.at[k]) for k, (x, y) in enumerate(pairs)]
    for copy in copies:
        copy.start()
    for copy in copies:
        copy.wait()


def shards(out_grad, routes, pre_act, out_weight, row_factor, col_factor):
    n_dp, n_e = lax.axis_size("dp"), lax.axis_size("expert")
    tok, d = out_grad.shape
    r = pre_act.shape[0]
    ff = out_weight.shape[1]
    slot = r // n_e
    packed = slot > 8
    assert slot <= 12
    kinds = 3 if packed else 1
    groups = 4
    chunk = next(c for c in (384, 256, 128) if ff % c == 0)
    deep = max(c for c in range(16, 257, 16) if d % c == 0)
    wide_d = up128(d) + d // 2 // 128 * 128 if packed else d
    assert not packed or 2 * d - d // 256 * 256 <= up128(d)
    wide_f = ff + ff // 2 if packed else ff
    row = np.arange(r)
    src, s = row // slot, row % slot
    q = np.zeros((kinds, r, n_e * 8), np.float32)
    low = s < 8
    q[0, row[low], (src * 8 + s)[low]] = 1
    if packed:
        q[1, row[~low], (src * 8 + s - 8)[~low]] = 1
        q[2, row[~low], (src * 8 + s - 4)[~low]] = 1
    qn = jnp.asarray(q, BF16)
    qt = jnp.asarray(q.transpose(0, 2, 1), BF16)
    vm = pl.BlockSpec(memory_space=pltpu.VMEM)
    hbm = pl.BlockSpec(memory_space=pl.ANY)
    dma = pltpu.SemaphoreType.DMA
    out = pltpu.VMEM
    hid, neww, newrow, newcol = pl.pallas_call(
        functools.partial(kernel, (n_dp, n_e, slot, groups, chunk, deep)),
        out_shape=(out((tok, ff * n_dp), BF16), out((1, d, ff), BF16),
                   out((1, ff), F32), out((1, d), F32)),
        in_specs=[vm, vm, hbm, hbm, vm, vm, vm, vm],
        out_specs=(vm, vm, vm, vm),
        scratch_shapes=[
            pltpu.VMEM((n_e, 8, wide_d), BF16),
            pltpu.VMEM((n_dp, n_e, 8, wide_d), BF16),
            pltpu.VMEM((n_dp, r, d), BF16),
            pltpu.VMEM((n_dp, r, ff), BF16),
            pltpu.VMEM((d, ff), BF16),
            pltpu.VMEM((d, ff), F32),
            pltpu.VMEM((n_dp, n_e, 8, wide_f), BF16),
            pltpu.VMEM((n_dp, n_e, 8, wide_f), BF16),
            pltpu.VMEM((n_dp, 2, d), F32),
            pltpu.VMEM((kinds, n_e * 8, tok), BF16),
            pltpu.VMEM((2, up128(d), 128), F32),
            pltpu.VMEM((1, up128(d)), F32),
            pltpu.VMEM((up128(d), 128), F32),
            dma((2,)), dma((n_e,)), dma((n_e,)),
            dma((n_dp, groups)), dma((n_dp, groups)), dma((n_dp,)), dma((n_dp,)),
            dma((n_dp, n_e)), dma((n_dp, n_e)), dma((n_dp,)), dma((n_dp,)),
        ],
        compiler_params=pltpu.CompilerParams(
            collective_id=0, has_side_effects=True, vmem_limit_bytes=59 * 1024 * 1024),
    )(out_grad.T, routes.reshape(1, tok), pre_act, jnp.swapaxes(out_weight, 1, 2), row_factor,
      col_factor, qn, qt)
    held = (hid, neww, newrow, newcol)
    hid, neww, newrow, newcol = pl.pallas_call(
        flush,
        out_shape=tuple(jax.ShapeDtypeStruct(x.shape, x.dtype) for x in held),
        in_specs=[vm] * 4,
        out_specs=[hbm] * 4,
        scratch_shapes=[dma((4,))],
        compiler_params=pltpu.CompilerParams(vmem_limit_bytes=1024 * 1024),
    )(*held)
    return hid, jnp.swapaxes(neww, 1, 2), newrow, newcol


def solution(mesh):
    placed = (
        P(("dp", "expert"), None),
        P(("dp", "expert"), None),
        P(("dp", "expert"), None),
        P("expert", "dp", None),
        P("expert", "dp"),
        P("expert", None),
    )
    return jax.shard_map(
        shards,
        mesh=mesh,
        in_specs=placed,
        out_specs=(
            P(("dp", "expert"), None),
            P("expert", "dp", None),
            P("expert", "dp"),
            P("expert", None),
        ),
        check_vma=False,
    )
```

```python
import functools
import jax
import jax.numpy as jnp
import numpy as np
from jax import lax
from jax.experimental import pallas as pl
from jax.experimental.pallas import tpu as pltpu
from jax.sharding import PartitionSpec as P

MESH = pl.DeviceIdType.MESH
F32, BF16 = jnp.float32, jnp.bfloat16


def up128(n):
    return -(-n // 128) * 128


def dot(a, b, ca=1, cb=0):
    return lax.dot_general(a, b, (((ca,), (cb,)), ((), ())), preferred_element_type=F32)


def onehot(hit):
    return jnp.where(hit, 1.0, 0.0).astype(BF16)


def kernel(cfg, og, rrow, pre, w, rf, cf, qn, qt,
           hid, neww, newrow, newcol,
           dy_out, dy_all, dyn, pre_all, wv, grad, snd, ret, colst, place, colacc, cspad, cscol,
           loc, dy_s, dy_r, fw_s, fw_r, pre_s, pre_r, rt_s, rt_r, st_s, st_r):
    n_dp, n_e, slot, groups, chunk, deep = cfg
    d, tok = og.shape
    ff = wv.shape[1]
    r = pre.shape[0]
    packed = slot > 8
    half, dp_off, h0 = ff // 2, up128(d), d // 2 // 128 * 128
    rest = d - 2 * h0
    g = n_e // groups
    i, e = lax.axis_index("dp"), lax.axis_index("expert")
    total = n_dp * n_e
    flat = i * n_e + e
    others = [lax.rem(i + o, n_dp) for o in range(1, n_dp)]

    barrier = pltpu.get_barrier_semaphore()

    def greet(k, _):
        t = lax.rem(flat + k, total)
        ti = lax.div(t, n_e)
        pl.semaphore_signal(barrier, inc=1, device_id=(ti, t - ti * n_e), device_id_type=MESH)
        return 0

    lax.fori_loop(1, total, greet, 0)

    get_w = pltpu.make_async_copy(w.at[0], wv, loc.at[0])
    cols = lambda t: pl.ds(pl.multiple_of(t * ff, 128), ff)
    get_pre = pltpu.make_async_copy(pre.at[:, cols(i)], pre_all.at[i], loc.at[1])
    get_w.start()
    get_pre.start()

    named = jnp.broadcast_to(rrow[...].astype(F32), (tok, tok))
    same = named == named.T
    at_row = lax.broadcasted_iota(jnp.int32, (tok, tok), 0)
    at_col = lax.broadcasted_iota(jnp.int32, (tok, tok), 1)
    order = jnp.sum(jnp.where(same & (at_row < at_col), 1.0, 0.0), axis=0, keepdims=True)
    base = rrow[...].astype(F32) * 8.0 + order
    rows = lax.broadcasted_iota(jnp.int32, (n_e * 8, tok), 0).astype(F32)
    place[0] = onehot(rows == jnp.where(order < 8.0, base, -1.0))
    dy_out[:, :, 0:d] = dot(place[0], og[...], 1, 1).reshape(n_e, 8, d).astype(BF16)
    if packed:
        place[1] = onehot(rows == jnp.where(order >= 8.0, base - 8.0, -1.0))
        place[2] = onehot(rows == jnp.where(order >= 8.0, base - 4.0, -1.0))
        tail = dot(place[1], og[0:h0, :], 1, 1) + dot(place[2], og[h0:2 * h0, :], 1, 1)
        dy_out[:, :, dp_off:dp_off + h0] = tail.reshape(n_e, 8, h0).astype(BF16)
        if rest:
            more = dot(place[1], og[2 * h0:d, :], 1, 1)
            dy_out[:, :, d:d + rest] = more.reshape(n_e, 8, rest).astype(BF16)

    side = n_e // 2
    near = lax.div(e, side)
    far = 1 - near

    def over(which, k):
        return which * side + lax.rem(e + k, side)

    def send_dy(t):
        return pltpu.make_async_remote_copy(
            src_ref=dy_out.at[t], dst_ref=dy_all.at[i, e], send_sem=dy_s.at[t],
            recv_sem=dy_r.at[e], device_id=(i, t), device_id_type=MESH)

    def send_pre(t):
        return pltpu.make_async_remote_copy(
            src_ref=pre.at[:, cols(t)], dst_ref=pre_all.at[i], send_sem=pre_s.at[t],
            recv_sem=pre_r.at[i], device_id=(t, e), device_id_type=MESH)

    def send_fw(t, q):
        part = pl.ds(q * g, g)
        return pltpu.make_async_remote_copy(
            src_ref=dy_all.at[i, part], dst_ref=dy_all.at[i, part], send_sem=fw_s.at[t, q],
            recv_sem=fw_r.at[i, q], device_id=(t, e), device_id_type=MESH)

    def send_ret(t, j):
        return pltpu.make_async_remote_copy(
            src_ref=snd.at[t, j], dst_ref=ret.at[i, e], send_sem=rt_s.at[t, j],
            recv_sem=rt_r.at[i, e], device_id=(t, j), device_id_type=MESH)

    def send_st(t):
        return pltpu.make_async_remote_copy(
            src_ref=colst.at[i], dst_ref=colst.at[i], send_sem=st_s.at[t],
            recv_sem=st_r.at[i], device_id=(t, e), device_id_type=MESH)

    def loop(n, act):
        def step(k, _):
            act(k)
            return 0
        lax.fori_loop(0, n, step, 0)

    def all_peers(act):
        loop(side, lambda k: act(over(far, k)))
        loop(side - 1, lambda k: act(over(near, k + 1)))

    pl.semaphore_wait(barrier, total - 1)
    for t in others:
        send_pre(t).start()
    all_peers(lambda t: send_dy(t).start())
    own = pltpu.make_async_copy(dy_out.at[e], dy_all.at[i, e], dy_r.at[e])
    own.start()

    colacc[...] = jnp.zeros_like(colacc)

    def receive(which):
        for k in range(groups // 2):
            q = which * (groups // 2) + k
            for m in range(g):
                j = q * g + m
                pltpu.make_async_copy(dy_out.at[0], dy_all.at[i, j], dy_r.at[j]).wait()
            for t in others:
                send_fw(t, q).start()

    def flat_rows(x):
        return x.astype(F32).reshape(x.shape[0] * 8, x.shape[2]).astype(BF16)

    def back(t, first, count):
        n = count * slot
        part = pl.ds(first, count)
        where = pl.ds(first * slot if isinstance(first, int) else pl.multiple_of(first * slot, 16), n)
        dy = dot(qn[0, 0:n, 0:count * 8], flat_rows(dy_all[t, part, :, 0:d]))
        if packed:
            q_lo, q_hi = qn[1, 0:n, 0:count * 8], qn[2, 0:n, 0:count * 8]
            tail = flat_rows(dy_all[t, part, :, dp_off:dp_off + h0])
            pieces = [dot(q_lo, tail), dot(q_hi, tail)]
            if rest:
                ends = dot(q_lo, flat_rows(dy_all[t, part, :, 2 * h0:dp_off]))
                pieces.append(ends[:, d - 2 * h0:d - 2 * h0 + rest])
            dy = dy + jnp.concatenate(pieces, axis=1)
        dy = dy.astype(BF16)
        dyn[t, where, :] = dy
        tail = None
        for c in range(2 if packed else 1):
            wide = half if packed else ff
            span = slice(c * wide, c * wide + wide)
            bk = dot(dy, wv[:, span])
            keep = pre_all[t, where, span].astype(F32) > 0.0
            bk = jnp.where(keep, bk, 0.0).astype(BF16)
            snd[t, part, :, span] = dot(qt[0, 0:count * 8, 0:n], bk).reshape(count, 8, wide).astype(BF16)
            if packed:
                more = dot(qt[1 + c, 0:count * 8, 0:n], bk)
                tail = more if tail is None else tail + more
        if packed:
            snd[t, part, :, ff:ff + half] = tail.reshape(count, 8, half).astype(BF16)

    receive(far)
    get_w.wait()
    get_pre.wait()
    back(i, far * side, side)
    loop(side, lambda k: send_ret(i, over(far, k)).start())
    receive(near)
    back(i, near * side, side)
    loop(side - 1, lambda k: send_ret(i, over(near, k + 1)).start())
    own_ret = pltpu.make_async_copy(snd.at[i, e], ret.at[i, e], rt_r.at[i, e])
    own_ret.start()

    def send_side(t, which):
        loop(side, lambda k: send_ret(t, over(which, k)).start())

    for t in others:
        pltpu.make_async_copy(pre_all.at[i], pre_all.at[t], pre_r.at[t]).wait()
        for which in (far, near):
            for k in range(groups // 2):
                q = which * (groups // 2) + k
                part = pl.ds(q * g, g)
                pltpu.make_async_copy(dy_all.at[i, part], dy_all.at[t, part], fw_r.at[t, q]).wait()
            back(t, which * side, side)
            if which is far:
                send_side(t, far)

    def gradient(c):
        span = pl.ds(pl.multiple_of(c * chunk, 128), chunk)
        acc = None
        for t in range(n_dp):
            part = dot(dyn[t], jnp.maximum(pre_all[t, :, span], 0), 0, 0)
            acc = part if acc is None else acc + part
        grad[:, span] = acc
        sq = acc * acc
        rn = 0.8 * rf[0:1, span] + 0.2 * (jnp.sum(sq, axis=0, keepdims=True) / d + 1e-30)
        newrow[0:1, span] = rn
        for k, x in enumerate((sq, sq * (1.0 / rn))):
            folded = x[:, 0:128]
            for b in range(1, chunk // 128):
                folded = folded + x[:, b * 128:b * 128 + 128]
            colacc[k, 0:d, :] += folded

    loop(ff // chunk, gradient)
    blocks = [(b, min(b + 128, d)) for b in range(0, d, 128)]
    for k in range(2):
        for lo, hi in blocks:
            sums = jnp.sum(colacc[k, lo:lo + 128, :].T, axis=0, keepdims=True)
            colst[i, k:k + 1, lo:hi] = sums[:, 0:hi - lo]
    for t in others:
        send_st(t).start()
        send_side(t, near)
    for t in others:
        pltpu.make_async_copy(colst.at[i], colst.at[t], st_r.at[t]).wait()
    col, weighted = jnp.zeros((1, d), F32), jnp.zeros((1, d), F32)
    for t in range(n_dp):
        col = col + colst[t, 0:1, :]
        weighted = weighted + colst[t, 1:2, :]
    full = ff * n_dp
    cn = 0.8 * cf[...] + 0.2 * (col / full + 1e-30)
    newcol[...] = cn
    spread = jnp.sqrt(jnp.sum(weighted / cn, axis=1, keepdims=True) / (full * d))
    cspad[...] = jnp.zeros_like(cspad)
    cspad[0:1, 0:d] = lax.rsqrt(cn) / jnp.maximum(1.0, spread / 0.01)
    for lo, hi in blocks:
        cscol[lo:lo + 128, :] = jnp.broadcast_to(cspad[0:1, lo:lo + 128], (128, 128)).T

    def apply(c):
        span = pl.ds(pl.multiple_of(c * deep, 16), deep)
        update = grad[span, :] * lax.rsqrt(newrow[...]) * cscol[span, 0:1]
        neww[0, span, :] = (wv[span, :].astype(F32) - update).astype(BF16)

    loop(d // deep, apply)

    for t in [i] + others:
        loop(n_e, lambda j: pltpu.make_async_copy(
            snd.at[0, 0], ret.at[t, j], rt_r.at[t, j]).wait())
        for c in range(2 if packed else 1):
            wide = half if packed else ff
            got = dot(place[0], flat_rows(ret[t, :, :, c * wide:c * wide + wide]), 0, 0)
            if packed:
                got = got + dot(place[1 + c], flat_rows(ret[t, :, :, ff:ff + half]), 0, 0)
            hid[:, pl.ds(pl.multiple_of(t * ff + c * wide, 128), wide)] = got.astype(BF16)

    all_peers(lambda t: send_dy(t).wait_send())
    all_peers(lambda t: send_ret(i, t).wait_send())
    for t in others:
        send_pre(t).wait_send()
        for q in range(groups):
            send_fw(t, q).wait_send()
        loop(n_e, lambda k: send_ret(t, k).wait_send())
        send_st(t).wait_send()


def flush(a, b, c, d, ao, bo, co, do, sem):
    pairs = ((b, bo), (a, ao), (c, co), (d, do))
    copies = [pltpu.make_async_copy(x, y, sem.at[k]) for k, (x, y) in enumerate(pairs)]
    for copy in copies:
        copy.start()
    for copy in copies:
        copy.wait()


def shards(out_grad, routes, pre_act, out_weight, row_factor, col_factor):
    n_dp, n_e = lax.axis_size("dp"), lax.axis_size("expert")
    tok, d = out_grad.shape
    r = pre_act.shape[0]
    ff = out_weight.shape[1]
    slot = r // n_e
    packed = slot > 8
    assert slot <= 12
    kinds = 3 if packed else 1
    groups = 4
    chunk = next(c for c in (384, 256, 128) if ff % c == 0)
    deep = max(c for c in range(16, 257, 16) if d % c == 0)
    wide_d = up128(d) + d // 2 // 128 * 128 if packed else d
    assert not packed or 2 * d - d // 256 * 256 <= up128(d)
    wide_f = ff + ff // 2 if packed else ff
    row = np.arange(r)
    src, s = row // slot, row % slot
    q = np.zeros((kinds, r, n_e * 8), np.float32)
    low = s < 8
    q[0, row[low], (src * 8 + s)[low]] = 1
    if packed:
        q[1, row[~low], (src * 8 + s - 8)[~low]] = 1
        q[2, row[~low], (src * 8 + s - 4)[~low]] = 1
    qn = jnp.asarray(q, BF16)
    qt = jnp.asarray(q.transpose(0, 2, 1), BF16)
    vm = pl.BlockSpec(memory_space=pltpu.VMEM)
    hbm = pl.BlockSpec(memory_space=pl.ANY)
    dma = pltpu.SemaphoreType.DMA
    out = pltpu.VMEM
    hid, neww, newrow, newcol = pl.pallas_call(
        functools.partial(kernel, (n_dp, n_e, slot, groups, chunk, deep)),
        out_shape=(out((tok, ff * n_dp), BF16), out((1, d, ff), BF16),
                   out((1, ff), F32), out((1, d), F32)),
        in_specs=[vm, vm, hbm, hbm, vm, vm, vm, vm],
        out_specs=(vm, vm, vm, vm),
        scratch_shapes=[
            pltpu.VMEM((n_e, 8, wide_d), BF16),
            pltpu.VMEM((n_dp, n_e, 8, wide_d), BF16),
            pltpu.VMEM((n_dp, r, d), BF16),
            pltpu.VMEM((n_dp, r, ff), BF16),
            pltpu.VMEM((d, ff), BF16),
            pltpu.VMEM((d, ff), F32),
            pltpu.VMEM((n_dp, n_e, 8, wide_f), BF16),
            pltpu.VMEM((n_dp, n_e, 8, wide_f), BF16),
            pltpu.VMEM((n_dp, 2, d), F32),
            pltpu.VMEM((kinds, n_e * 8, tok), BF16),
            pltpu.VMEM((2, up128(d), 128), F32),
            pltpu.VMEM((1, up128(d)), F32),
            pltpu.VMEM((up128(d), 128), F32),
            dma((2,)), dma((n_e,)), dma((n_e,)),
            dma((n_dp, groups)), dma((n_dp, groups)), dma((n_dp,)), dma((n_dp,)),
            dma((n_dp, n_e)), dma((n_dp, n_e)), dma((n_dp,)), dma((n_dp,)),
        ],
        compiler_params=pltpu.CompilerParams(
            collective_id=0, has_side_effects=True, vmem_limit_bytes=59 * 1024 * 1024),
    )(out_grad.T, routes.reshape(1, tok), pre_act, jnp.swapaxes(out_weight, 1, 2), row_factor,
      col_factor, qn, qt)
    held = (hid, neww, newrow, newcol)
    hid, neww, newrow, newcol = pl.pallas_call(
        flush,
        out_shape=tuple(jax.ShapeDtypeStruct(x.shape, x.dtype) for x in held),
        in_specs=[vm] * 4,
        out_specs=[hbm] * 4,
        scratch_shapes=[dma((4,))],
        compiler_params=pltpu.CompilerParams(vmem_limit_bytes=1024 * 1024),
    )(*held)
    return hid, jnp.swapaxes(neww, 1, 2), newrow, newcol


def solution(mesh):
    placed = (
        P(("dp", "expert"), None),
        P(("dp", "expert"), None),
        P(("dp", "expert"), None),
        P("expert", "dp", None),
        P("expert", "dp"),
        P("expert", None),
    )
    return jax.shard_map(
        shards,
        mesh=mesh,
        in_specs=placed,
        out_specs=(
            P(("dp", "expert"), None),
            P("expert", "dp", None),
            P("expert", "dp"),
            P("expert", None),
        ),
        check_vma=False,
    )
```
